32 devices in a mesh: groups: 2 (over y), seq: 4 (over z), head: 4 (over x, core).
Axes of the slice: x: 2, y: 2, z: 4, core: 2. Of those that a mesh axis runs over, the one named last changes fastest.
Arguments:
- tokens: bfloat16 [8192, 2048], P(('groups', 'seq'), 'head'), parts along dimension 0, may hold values from -6 to 6
- q_weight: bfloat16 [2048, 2048], P(None, 'head'), may hold values from -0.125 to 0.125
- k_weight: bfloat16 [2048, 2048], P(None, 'head'), may hold values from -0.125 to 0.125
- v_weight: bfloat16 [2048, 2048], P(None, 'head'), may hold values from -0.125 to 0.125
- level_table: float32 [16, 16], P('head'), may hold values from 0.1 to 1
- level_index: int32 [6, 8192], P(None, ('groups', 'seq')), parts along dimension 1, may hold values from 0 to 15
- out_gain: float32 [2048], P('head'), may hold values from 0.5 to 1.5
Outputs:
- attended: bfloat16 [8192, 2048], P(('groups', 'seq'), 'head'), parts along dimension 0
The draws below stay inside these ranges and needn't reach their ends.
There are 2 independent parts, one for each index of `groups`. The reference program is written for one: setup_inputs(seed, part) draws one part's arguments, and reference() takes and returns one part's arrays. A program takes and returns all parts, laid end to end along the dimension named above; an argument that names none is the same for every part. Nothing has to cross between parts.
Inputs may be any that keep to these rules, and one draw needn't show every extreme that they name: `level_index`: row 0 weights a token's own block, row l + 1 its level-l merged state.
All inputs are finite; a program needn't handle non-finite values.
Results may differ from the reference program's by a relative error of at most 0.012.
Values may be sent and summed in bfloat16 or wider, within the bound.
No kernel may reach another device: no remote copies, remote signals or barrier semaphores. Data moves between devices by JAX's collectives and lax.ppermute only.
A program may use at most 64 MiB of HBM per device.

```python
import math
import jax
import jax.numpy as jnp
from jax import lax

D = 2048
HEADS = 16
HD = 128
TOK_DEV = 1024
LEVELS = 5
QLEV = 16
TOKENS = 4096
N_SEQ = 4


def set_ends(entries, key, least, largest):
    spot = [jax.random.randint(jax.random.fold_in(key, axis), (), 0, length) for axis, length in enumerate(entries.shape)]
    longest = entries.shape.index(max(entries.shape))
    beside = spot[:longest] + [(spot[longest] + 1) % entries.shape[longest]] + spot[longest + 1:]
    return entries.at[tuple(spot)].set(least).at[tuple(beside)].set(largest)


def block_levels(own_key, extent, split, least, top_value):
    factor_of, own = 1.0, jax.random.fold_in(own_key, 6)
    for dim, blocks in split:
        steps = jnp.exp(jax.random.uniform(jax.random.fold_in(own, dim), (blocks,), jnp.float32, least / len(split), top_value / len(split)))
        factor_of = factor_of * jnp.repeat(steps, extent[dim] // blocks).reshape([-1 if axis == dim else 1 for axis in range(len(extent))])
    return factor_of


def noise(key, extent, spread, limit, cuts=(), kind=jnp.bfloat16):
    result = jax.random.normal(key, extent, jnp.float32) * spread
    if len(cuts) > 0:
        result = block_levels(key, extent, cuts, -0.22, 0.18) * result
    return jnp.clip(result, min=-limit, max=limit).astype(kind)


def setup_inputs(seed: int = 0, part: int = 0) -> dict:
    splits = jax.random.split(jax.random.key(seed), 8)
    part_splits = jax.random.split(jax.random.fold_in(splits[7], part), 8)
    tokens = noise(part_splits[0], (TOKENS, D), 1.0, 6.0, ((0, 4), (1, 4)))
    q_weight = noise(splits[1], (D, HEADS * HD), D ** -0.5, 0.125, ((1, 4),))
    k_weight = noise(splits[2], (D, HEADS * HD), D ** -0.5, 0.125, ((1, 4),))
    v_weight = noise(splits[3], (D, HEADS * HD), D ** -0.5, 0.125, ((1, 4),))
    level_table = jnp.clip(jnp.exp(math.log(1.0) - 2.3025851 * jax.random.uniform(splits[4], (HEADS, QLEV), jnp.float32) ** block_levels(splits[4], (HEADS, QLEV), ((0, 4),), -0.2, 0.2)), 0.1, 1.0)
    level_index = set_ends(jax.random.randint(part_splits[5], (LEVELS + 1, TOKENS), 0, QLEV), jax.random.fold_in(part_splits[5], 1), 0, QLEV - 1).astype(jnp.int32)
    out_gain = jnp.clip(1.0 + 0.1 * jax.random.normal(splits[6], (HEADS * HD,), jnp.float32), 0.5, 1.5)
    return {"tokens": tokens, "q_weight": q_weight, "k_weight": k_weight, "v_weight": v_weight, "level_table": level_table, "level_index": level_index, "out_gain": out_gain}


def unit_norm(raw_rows):
    return (raw_rows / jnp.sqrt(lax.optimization_barrier(jnp.sum(raw_rows * raw_rows, -1, keepdims=True)) + 1e-06)).astype(jnp.bfloat16)

def reference(tokens, q_weight, k_weight, v_weight, level_table, level_index, out_gain):

    def project(weight):
        return jnp.dot(tokens, weight, preferred_element_type=jnp.float32).reshape(TOKENS, HEADS, HD)
    queries = unit_norm(project(q_weight)).reshape(N_SEQ, TOK_DEV, HEADS, HD)
    key_rows = unit_norm(project(k_weight)).reshape(N_SEQ, TOK_DEV, HEADS, HD)
    values = project(v_weight).astype(jnp.bfloat16).reshape(N_SEQ, TOK_DEV, HEADS, HD)
    kv_state = jnp.einsum('bthd,bthe->bhde', key_rows.astype(jnp.float32), values.astype(jnp.float32))
    one_hot = (level_index[:, :, None] == jnp.arange(QLEV, dtype=jnp.int32)[None, None, :]).astype(jnp.float32)
    level_weight = jnp.einsum('ltq,hq->lth', one_hot, level_table, precision=lax.Precision.HIGHEST)
    level_weight = level_weight.reshape(LEVELS + 1, N_SEQ, TOK_DEV, HEADS).transpose(1, 0, 2, 3)
    block_ids = jnp.arange(N_SEQ, dtype=jnp.int32)
    level_span = (2 ** jnp.arange(LEVELS, dtype=jnp.int32)).astype(jnp.int32)
    causal = jnp.arange(TOK_DEV)[:, None] >= jnp.arange(TOK_DEV)[None, :]
    gain_rows = out_gain.reshape(HEADS, HD)

    def one_block(inputs):
        block_q, block_k, block_v, weights_here, block_id = inputs
        scores = jnp.einsum('thd,shd->hts', block_q.astype(jnp.float32), block_k.astype(jnp.float32))
        scores = jnp.where(causal[None], scores, 0.0).astype(jnp.bfloat16)
        local_term = jnp.einsum('hts,shd->thd', scores.astype(jnp.float32), block_v.astype(jnp.float32))
        low_edge = block_id // (2 * level_span) * (2 * level_span)
        high_edge = block_id // level_span * level_span
        membership = ((block_ids[None, :] >= low_edge[:, None]) & (block_ids[None, :] < high_edge[:, None])).astype(jnp.float32)
        merged = jnp.einsum('lc,chde->lhde', membership, kv_state, precision=lax.Precision.HIGHEST)
        scaled = block_q.astype(jnp.float32)[None] * weights_here[1:, :, :, None]
        far_term = jnp.einsum('lthd,lhde->the', scaled, merged, precision=lax.Precision.HIGHEST)
        combined = weights_here[0][:, :, None] * local_term + far_term
        normalized = combined / jnp.sqrt(lax.optimization_barrier(jnp.mean(combined * combined, -1, keepdims=True)) + 1e-06) * gain_rows
        return normalized.astype(jnp.bfloat16)
    attended = lax.map(one_block, (queries, key_rows, values, level_weight, block_ids))
    return attended.reshape(TOKENS, HEADS * HD)
```

```python
import functools

import jax
import jax.numpy as jnp
from jax import lax
from jax.experimental import pallas as pl
from jax.experimental.pallas import tpu as pltpu
from jax.sharding import PartitionSpec as P

LEVELS = 5
CHUNKS = (2, 2, 2, 1, 1)
EPS = 1e-06
F32 = jnp.float32
BF16 = jnp.bfloat16


def swap(block, axis, apart):
    route = [(i, i ^ apart) for i in range(lax.axis_size(axis))]
    return lax.ppermute(block, axis, route)


def dot(a, b, dims=((1,), (0,))):
    return lax.dot_general(a, b, (dims, ((), ())), preferred_element_type=F32)


def project(me, pieces, weight):
    depth = pieces[0].shape[1]
    total = None
    for offset, piece in enumerate(pieces):
        rows = pl.multiple_of((me ^ offset) * depth, depth)
        part = dot(piece[...], weight[pl.ds(rows, depth), :])
        total = part if total is None else total + part
    return total


def unit_rows(raw):
    return (raw * lax.rsqrt(jnp.sum(raw * raw, -1, keepdims=True) + EPS)).astype(BF16)


def kv_kernel(n_pieces, heads, me, *refs):
    pieces = refs[:n_pieces]
    k_weight, v_weight, state_in, keys, values, state, state_low = refs[n_pieces:]
    size = k_weight.shape[1] // heads
    raw_k = project(me[0], pieces, k_weight)
    raw_v = project(me[0], pieces, v_weight).astype(BF16)
    values[...] = raw_v
    for head in range(heads):
        cols = slice(head * size, (head + 1) * size)
        key = unit_rows(raw_k[:, cols])
        keys[:, cols] = key
        total = state_in[head] + dot(key, raw_v[:, cols], ((0,), (0,)))
        state[head] = total
        state_low[head] = total.astype(BF16)


def query_kernel(n_pieces, heads, depth, me, bits, *refs):
    pieces = refs[:n_pieces]
    q_weight, keys, values, state_in, index, table, part = refs[n_pieces : n_pieces + 7]
    scaled = refs[n_pieces + 7 :]
    size = q_weight.shape[1] // heads
    rows = keys.shape[0]
    quant = table.shape[0] // 2
    levels = index.shape[0]
    spot = lax.broadcasted_iota(jnp.int32, (quant, rows), 0)

    def picked(level):
        return (index[level : level + 1, :] == spot).astype(F32)

    def weigh(hot):
        hot = hot.astype(BF16)
        return dot(jnp.concatenate([hot, hot], 0), table[...], ((0,), (0,)))

    own = weigh(picked(0))
    far = [weigh(picked(level + 1)) for level in range(depth)]
    rest = functools.reduce(jnp.add, [picked(level) for level in range(depth + 1, levels)], jnp.zeros((quant, rows), F32))
    rest = weigh(rest)
    raw_q = project(me[0], pieces, q_weight)
    causal = lax.broadcasted_iota(jnp.int32, (rows, rows), 0) >= lax.broadcasted_iota(jnp.int32, (rows, rows), 1)
    for head in range(heads):
        cols = slice(head * size, (head + 1) * size)
        query = unit_rows(raw_q[:, cols])
        scores = dot(query, keys[:, cols], ((1,), (1,)))
        scores = jnp.where(causal, scores, 0.0).astype(BF16)
        local = dot(scores, values[:, cols]) + dot(query, state_in[head].astype(BF16))
        wide = query.astype(F32)
        empty = (wide * rest[:, cols]).astype(BF16)
        local = own[:, cols] * local + dot(empty, jnp.zeros((size, size), BF16))
        part[:, cols] = local
        for level in range(depth):
            scale = far[level][:, cols] * bits[level].astype(F32)
            scaled[level][:, cols] = (wide * scale).astype(BF16)


def final_kernel(heads, depth, part, *refs):
    scaled = refs[:depth]
    merged = refs[depth : 2 * depth]
    gain, out = refs[2 * depth :]
    size = part.shape[1] // heads
    for head in range(heads):
        cols = slice(head * size, (head + 1) * size)
        total = part[:, cols]
        for level in range(depth):
            total = total + dot(scaled[level][:, cols], merged[level][head])
        total = total * lax.rsqrt(jnp.mean(total * total, -1, keepdims=True) + EPS)
        out[:, cols] = (total * gain[0:1, cols]).astype(BF16)


VMEM = pl.BlockSpec(memory_space=pltpu.VMEM)
SMEM = pl.BlockSpec(memory_space=pltpu.SMEM)


def on_device(tokens, q_weight, k_weight, v_weight, level_table, level_index, out_gain):
    row_count, feat_here = tokens.shape
    width = q_weight.shape[1]
    heads, quant = level_table.shape
    size = width // heads
    n_head = lax.axis_size("head")
    depth = lax.axis_size("seq").bit_length() - 1
    me = lax.axis_index("head").astype(jnp.int32).reshape(1)
    block = lax.axis_index("seq")
    bits = jnp.stack([(block >> level & 1).astype(jnp.int32) for level in range(depth)] + [jnp.int32(0)])

    unit = row_count // sum(CHUNKS)
    edges = [0]
    for share in CHUNKS:
        edges.append(edges[-1] + share * unit)

    top = n_head // 2
    chunk_pieces = []
    for lo, hi in zip(edges[:-1], edges[1:]):
        pieces = {0: tokens[lo:hi]}
        apart = top
        while apart:
            for offset in sorted(pieces):
                pieces[offset | apart] = swap(pieces[offset], "head", apart)
            apart //= 2
        chunk_pieces.append([pieces[o] for o in range(n_head)])

    table = jnp.repeat(level_table.T, size, axis=1)
    high = table.astype(BF16)
    table = jnp.concatenate([high, (table - high.astype(F32)).astype(BF16)], 0)

    params = pltpu.CompilerParams(vmem_limit_bytes=48 << 20)
    state = jnp.zeros((heads, size, size), F32)
    shape = jax.ShapeDtypeStruct
    queued = []
    for lo, hi, pieces in zip(edges[:-1], edges[1:], chunk_pieces):
        rows = hi - lo
        keys, values, new_state, state_low = pl.pallas_call(
            functools.partial(kv_kernel, n_head, heads),
            out_shape=[shape((rows, width), BF16)] * 2
            + [shape((heads, size, size), F32), shape((heads, size, size), BF16)],
            in_specs=[SMEM] + [VMEM] * (n_head + 3),
            out_specs=[VMEM] * 4,
            compiler_params=params,
            name="kv",
        )(me, *pieces, k_weight, v_weight, state)
        queued.append((lo, hi, pieces, keys, values, state))
        state = new_state

    merged = []
    group_sum = state
    for level in range(depth):
        sent = state_low if level == 0 else group_sum.astype(BF16)
        partner = swap(sent, "seq", 1 << level)
        merged.append(partner)
        group_sum = group_sum + partner.astype(F32)

    parts = []
    scaled = []
    for lo, hi, pieces, keys, values, before in queued:
        rows = hi - lo
        outs = pl.pallas_call(
            functools.partial(query_kernel, n_head, heads, depth),
            out_shape=[shape((rows, width), F32)] + [shape((rows, width), BF16)] * depth,
            in_specs=[SMEM, SMEM] + [VMEM] * (n_head + 6),
            out_specs=[VMEM] * (1 + depth),
            compiler_params=params,
            name="query",
        )(me, bits, *pieces, q_weight, keys, values, before, level_index[:, lo:hi], table)
        parts.append(outs[0])
        scaled.append(outs[1:])

    outs = []
    for part, scale in zip(parts, scaled):
        outs.append(
            pl.pallas_call(
                functools.partial(final_kernel, heads, depth),
                out_shape=shape(part.shape, BF16),
                in_specs=[VMEM] * (2 + 2 * depth),
                out_specs=VMEM,
                compiler_params=params,
                name="final",
            )(part, *scale, *merged, out_gain.reshape(1, width))
        )
    return jnp.concatenate(outs, 0)


def solution(mesh):
    return jax.shard_map(
        on_device,
        mesh=mesh,
        in_specs=(
            P(("groups", "seq"), "head"),
            P(None, "head"),
            P(None, "head"),
            P(None, "head"),
            P("head", None),
            P(None, ("groups", "seq")),
            P("head"),
        ),
        out_specs=P(("groups", "seq"), "head"),
        check_vma=False,
    )
```

```python
import functools

import jax
import jax.numpy as jnp
from jax import lax
from jax.experimental import pallas as pl
from jax.experimental.pallas import tpu as pltpu
from jax.sharding import PartitionSpec as P


CHUNKS = (2, 2, 2, 1, 1)
EPS = 1e-06
F32 = jnp.float32
BF16 = jnp.bfloat16
VMEM = pl.BlockSpec(memory_space=pltpu.VMEM)
SMEM = pl.BlockSpec(memory_space=pltpu.SMEM)
ANY = pl.BlockSpec(memory_space=pl.ANY)


def swap(block, axis, apart):
    route = [(i, i ^ apart) for i in range(lax.axis_size(axis))]
    return lax.ppermute(block, axis, route)


def dot(a, b, dims=((1,), (0,))):
    return lax.dot_general(a, b, (dims, ((), ())), preferred_element_type=F32)


def call(kernel, outs, in_specs, args, out_specs=None, scratch=(), limit=8):
    return pl.pallas_call(
        kernel,
        out_shape=[jax.ShapeDtypeStruct(*out) for out in outs],
        in_specs=in_specs,
        out_specs=out_specs or [VMEM] * len(outs),
        scratch_shapes=scratch,
        compiler_params=pltpu.CompilerParams(vmem_limit_bytes=limit << 20),
    )(*args)


def weight_rows(me, weight, offset, depth):
    start = pl.multiple_of((me ^ offset) * depth, depth)
    return weight[pl.ds(start, depth), :]


def unit_rows(raw):
    return (raw * lax.rsqrt(jnp.sum(raw * raw, -1, keepdims=True) + EPS)).astype(BF16)


def cut_kernel(spans, tokens, *refs):
    count = len(spans)
    outs, sems = refs[:count], refs[count]
    copies = []
    for i, (lo, hi) in enumerate(spans):
        copy = pltpu.make_async_copy(tokens.at[lo:hi], outs[i], sems.at[i])
        copy.start()
        copies.append(copy)
    for copy in copies:
        copy.wait()


def early_kernel(n_near, tile, me, *refs):
    pieces = refs[:n_near]
    weights = refs[n_near : n_near + 3]
    sums = refs[n_near + 3 :]
    rows, depth = pieces[0].shape

    def step(i, carry):
        at = pl.ds(pl.multiple_of(i * tile, tile), tile)
        for weight, total in zip(weights, sums):
            acc = None
            for offset, piece in enumerate(pieces):
                part = dot(piece[at, :], weight_rows(me[0], weight, offset, depth))
                acc = part if acc is None else acc + part
            total[at, :] = acc
        return carry

    lax.fori_loop(0, rows // tile, step, 0)


def late_sum(me, base, pieces, weight, early, lo, rows):
    depth = pieces[0].shape[1]
    acc = early[lo : lo + rows, :]
    for offset, piece in enumerate(pieces):
        acc = acc + dot(piece[...], weight_rows(me, weight, base + offset, depth))
    return acc


def kv_kernel(base, lo, heads, me, *refs):
    pieces = refs[:base]
    k_weight, v_weight, k_early, v_early = refs[base : base + 4]
    state_in = refs[base + 4] if lo else None
    keys, values, state, state_low = refs[-4:]
    rows, width = keys.shape
    size = width // heads
    raw_v = late_sum(me[0], base, pieces, v_weight, v_early, lo, rows).astype(BF16)
    values[...] = raw_v
    raw_k = late_sum(me[0], base, pieces, k_weight, k_early, lo, rows)
    for head in range(heads):
        cols = slice(head * size, (head + 1) * size)
        key = unit_rows(raw_k[:, cols])
        keys[:, cols] = key
        total = dot(key, raw_v[:, cols], ((0,), (0,)))
        if lo:
            total = state_in[head] + total
        state[head] = total
        state_low[head] = total.astype(BF16)


def table_kernel(table, wide):
    heads, _ = table.shape
    width = wide.shape[1]
    size = width // heads
    row = lax.broadcasted_iota(jnp.int32, (heads, width), 0)
    col = lax.broadcasted_iota(jnp.int32, (heads, width), 1)
    mine = ((col >= row * size) & (col < (row + 1) * size)).astype(BF16)
    exact = table[...]
    high = exact.astype(BF16)
    low = (exact - high.astype(F32)).astype(BF16)
    both = [dot(part, mine, ((0,), (0,))).astype(BF16) for part in (high, low)]
    wide[...] = jnp.concatenate(both, 0)


def level_weights(depth, block, index, table):
    quant = table.shape[0] // 2
    levels, rows = index.shape
    spot = lax.broadcasted_iota(jnp.int32, (quant, rows), 0)

    def picked(level):
        return (index[level : level + 1, :] == spot).astype(F32)

    def weigh(hot):
        hot = hot.astype(BF16)
        return dot(jnp.concatenate([hot, hot], 0), table[...], ((0,), (0,)))

    rest = jnp.zeros((quant, rows), F32)
    for level in range(depth + 1, levels):
        rest = rest + picked(level)
    far = [weigh(picked(level + 1)) * (block >> level & 1).astype(F32) for level in range(depth)]
    return weigh(picked(0)), weigh(rest), far


def query_kernel(base, lo, heads, depth, me, block, *refs):
    pieces = refs[:base]
    q_weight, q_early, keys, values, index, table = refs[base : base + 6]
    state_in = refs[base + 6] if lo else None
    part = refs[-1 - depth]
    scaled = refs[-depth:]
    rows, width = keys.shape
    size = width // heads
    own, rest, far = level_weights(depth, block[0], index[:, lo : lo + rows], table)
    raw_q = late_sum(me[0], base, pieces, q_weight, q_early, lo, rows)
    causal = lax.broadcasted_iota(jnp.int32, (rows, rows), 0) >= lax.broadcasted_iota(jnp.int32, (rows, rows), 1)
    for head in range(heads):
        cols = slice(head * size, (head + 1) * size)
        query = unit_rows(raw_q[:, cols])
        scores = dot(query, keys[:, cols], ((1,), (1,)))
        scores = jnp.where(causal, scores, 0.0).astype(BF16)
        local = dot(scores, values[:, cols])
        if lo:
            local = local + dot(query, state_in[head].astype(BF16))
        wide = query.astype(F32)
        empty = (wide * rest[:, cols]).astype(BF16)
        part[:, cols] = own[:, cols] * local + dot(empty, jnp.zeros((size, size), BF16))
        for level in range(depth):
            scaled[level][:, cols] = (wide * far[level][:, cols]).astype(BF16)


def add_kernel(total, partner, grown, low):
    summed = total[...] + partner[...].astype(F32)
    grown[...] = summed
    low[...] = summed.astype(BF16)


def final_kernel(heads, depth, edges, *refs):
    count = len(edges) - 1
    parts = refs[:count]
    scaled = [refs[count * (1 + level) : count * (2 + level)] for level in range(depth)]
    refs = refs[count * (1 + depth) :]
    merged = refs[:depth]
    gain, out, done, sems = refs[depth:]
    size = done.shape[1] // heads
    copies = []
    for i in range(count):
        rows = slice(edges[i], edges[i + 1])
        for head in range(heads):
            cols = slice(head * size, (head + 1) * size)
            total = parts[i][:, cols]
            for level in range(depth):
                total = total + dot(scaled[level][i][:, cols], merged[level][head])
            total = total * lax.rsqrt(jnp.mean(total * total, -1, keepdims=True) + EPS)
            done[rows, cols] = (total * gain[0:1, cols]).astype(BF16)
        copy = pltpu.make_async_copy(done.at[rows], out.at[rows], sems.at[i])
        copy.start()
        copies.append(copy)
    for copy in copies:
        copy.wait()


def hop(piece, base):
    pieces = [piece]
    apart = 1
    while apart < base:
        pieces += [swap(piece, "head", apart) for piece in pieces]
        apart *= 2
    return pieces


def on_device(tokens, q_weight, k_weight, v_weight, level_table, level_index, out_gain):
    row_count, feat_here = tokens.shape
    width = q_weight.shape[1]
    heads, quant = level_table.shape
    size = width // heads
    base = lax.axis_size("head") // 2
    depth = lax.axis_size("seq").bit_length() - 1
    me = lax.axis_index("head").astype(jnp.int32).reshape(1)
    block = lax.axis_index("seq").astype(jnp.int32).reshape(1)

    unit = row_count // sum(CHUNKS)
    edges = [0]
    for share in CHUNKS:
        edges.append(edges[-1] + share * unit)
    spans = list(zip(edges[:-1], edges[1:]))

    cuts = []
    for group in (spans[:1], spans[1:]):
        cuts += call(
            functools.partial(cut_kernel, group),
            [((hi - lo, feat_here), BF16) for lo, hi in group],
            [ANY],
            (tokens,),
            scratch=[pltpu.SemaphoreType.DMA((len(group),))],
        )
    far = [swap(piece, "head", base) for piece in cuts]
    near = hop(tokens, base)

    big = (row_count, width)
    early = call(
        functools.partial(early_kernel, base, row_count // 4),
        [(big, F32)] * 3,
        [SMEM] + [VMEM] * (base + 3),
        (me, *near, q_weight, k_weight, v_weight),
    )
    table = call(table_kernel, [((2 * quant, width), BF16)], [VMEM], (level_table,))[0]

    state = []
    parts = []
    scaled = []
    for i, (lo, hi) in enumerate(spans):
        rows = hi - lo
        pieces = hop(far[i], base)
        before = state
        args = (me, *pieces, k_weight, v_weight, early[1], early[2], *before)
        keys, values, total, low = call(
            functools.partial(kv_kernel, base, lo, heads),
            [((rows, width), BF16)] * 2 + [((heads, size, size), F32), ((heads, size, size), BF16)],
            [SMEM] + [VMEM] * (len(args) - 1),
            args,
        )
        state = [total]
        args = (me, block, *pieces, q_weight, early[0], keys, values, level_index, table, *before)
        outs = call(
            functools.partial(query_kernel, base, lo, heads, depth),
            [((rows, width), F32)] + [((rows, width), BF16)] * depth,
            [SMEM, SMEM] + [VMEM] * (len(args) - 2),
            args,
        )
        parts.append(outs[0])
        scaled.append(outs[1:])

    merged = []
    for level in range(depth):
        partner = swap(low, "seq", 1 << level)
        merged.append(partner)
        if level + 1 < depth:
            shape = (heads, size, size)
            total, low = call(add_kernel, [(shape, F32), (shape, BF16)], [VMEM, VMEM], (total, partner))

    inputs = parts + [chunk[level] for level in range(depth) for chunk in scaled] + merged
    return call(
        functools.partial(final_kernel, heads, depth, edges),
        [(big, BF16)],
        [VMEM] * (len(inputs) + 1),
        (*inputs, out_gain.reshape(1, width)),
        out_specs=[ANY],
        scratch=[pltpu.VMEM(big, BF16), pltpu.SemaphoreType.DMA((len(spans),))],
    )[0]


def solution(mesh):
    return jax.shard_map(
        on_device,
        mesh=mesh,
        in_specs=(
            P(("groups", "seq"), "head"),
            P(None, "head"),
            P(None, "head"),
            P(None, "head"),
            P("head", None),
            P(None, ("groups", "seq")),
            P("head"),
        ),
        out_specs=P(("groups", "seq"), "head"),
        check_vma=False,
    )
```

```python
import functools

import jax
import jax.numpy as jnp
from jax import lax
from jax.experimental import pallas as pl
from jax.experimental.pallas import tpu as pltpu
from jax.sharding import PartitionSpec as P


CHUNKS = (2, 2, 2, 1, 1)
EPS = 1e-06
F32 = jnp.float32
BF16 = jnp.bfloat16
VMEM = pl.BlockSpec(memory_space=pltpu.VMEM)
ANY = pl.BlockSpec(memory_space=pl.ANY)


def swap(block, axis, apart):
    route = [(i, i ^ apart) for i in range(lax.axis_size(axis))]
    return lax.ppermute(block, axis, route)


def dot(a, b, dims=((1,), (0,))):
    return lax.dot_general(a, b, (dims, ((), ())), preferred_element_type=F32)


def keep(array):
    return pltpu.with_memory_space_constraint(array, pltpu.VMEM)


def call(kernel, outs, in_specs, args, out_specs=None, scratch=(), limit=8):
    kept = [pltpu.VMEM(*out) for out in outs]
    return pl.pallas_call(
        kernel,
        out_shape=kept if out_specs is None else [jax.ShapeDtypeStruct(*out) for out in outs],
        in_specs=in_specs,
        out_specs=out_specs or [VMEM] * len(outs),
        scratch_shapes=scratch,
        compiler_params=pltpu.CompilerParams(vmem_limit_bytes=limit << 20),
    )(*args)


def weight_rows(me, weight, offset, depth):
    start = pl.multiple_of((me ^ offset) * depth, depth)
    return weight[pl.ds(start, depth), :]


def unit_rows(raw):
    return (raw * lax.rsqrt(jnp.sum(raw * raw, -1, keepdims=True) + EPS)).astype(BF16)


def cut_kernel(spans, tokens, *refs):
    count = len(spans)
    outs, sems = refs[:count], refs[count]
    copies = []
    for i, (lo, hi) in enumerate(spans):
        copy = pltpu.make_async_copy(tokens.at[lo:hi], outs[i], sems.at[i])
        copy.start()
        copies.append(copy)
    for copy in copies:
        copy.wait()


def early_kernel(n_near, tile, *refs):
    me = lax.axis_index("head")
    pieces = refs[:n_near]
    weights = refs[n_near : n_near + 3]
    sums = refs[n_near + 3 :]
    rows, depth = pieces[0].shape

    def step(i, carry):
        at = pl.ds(pl.multiple_of(i * tile, tile), tile)
        for weight, total in zip(weights, sums):
            acc = None
            for offset, piece in enumerate(pieces):
                part = dot(piece[at, :], weight_rows(me, weight, offset, depth))
                acc = part if acc is None else acc + part
            total[at, :] = acc
        return carry

    lax.fori_loop(0, rows // tile, step, 0)


def late_sum(base, pieces, weight, early, lo, rows):
    me = lax.axis_index("head")
    depth = pieces[0].shape[1]
    acc = early[lo : lo + rows, :]
    for offset, piece in enumerate(pieces):
        acc = acc + dot(piece[...], weight_rows(me, weight, base + offset, depth))
    return acc


def kv_kernel(base, lo, heads, *refs):
    pieces = refs[:base]
    k_weight, v_weight, k_early, v_early = refs[base : base + 4]
    state_in = refs[base + 4] if lo else None
    keys, values, state, state_low = refs[-4:]
    rows, width = keys.shape
    size = width // heads
    raw_v = late_sum(base, pieces, v_weight, v_early, lo, rows).astype(BF16)
    values[...] = raw_v
    raw_k = late_sum(base, pieces, k_weight, k_early, lo, rows)
    for head in range(heads):
        cols = slice(head * size, (head + 1) * size)
        key = unit_rows(raw_k[:, cols])
        keys[:, cols] = key
        total = dot(key, raw_v[:, cols], ((0,), (0,)))
        if lo:
            total = state_in[head] + total
        state[head] = total
        state_low[head] = total.astype(BF16)


def table_kernel(table, wide):
    heads, _ = table.shape
    width = wide.shape[1]
    size = width // heads
    row = lax.broadcasted_iota(jnp.int32, (heads, width), 0)
    col = lax.broadcasted_iota(jnp.int32, (heads, width), 1)
    mine = ((col >= row * size) & (col < (row + 1) * size)).astype(BF16)
    exact = table[...]
    high = exact.astype(BF16)
    low = (exact - high.astype(F32)).astype(BF16)
    both = [dot(part, mine, ((0,), (0,))).astype(BF16) for part in (high, low)]
    wide[...] = jnp.concatenate(both, 0)


def level_weights(depth, block, index, table):
    quant = table.shape[0] // 2
    levels, rows = index.shape
    spot = lax.broadcasted_iota(jnp.int32, (quant, rows), 0)

    def picked(level):
        return (index[level : level + 1, :] == spot).astype(F32)

    def weigh(hot):
        hot = hot.astype(BF16)
        return dot(jnp.concatenate([hot, hot], 0), table[...], ((0,), (0,)))

    rest = jnp.zeros((quant, rows), F32)
    for level in range(depth + 1, levels):
        rest = rest + picked(level)
    far = [weigh(picked(level + 1)) * (block >> level & 1).astype(F32) for level in range(depth)]
    return weigh(picked(0)), weigh(rest), far


def query_kernel(base, lo, heads, depth, *refs):
    pieces = refs[:base]
    q_weight, q_early, keys, values, index, table = refs[base : base + 6]
    state_in = refs[base + 6] if lo else None
    part = refs[-1 - depth]
    scaled = refs[-depth:]
    rows, width = keys.shape
    size = width // heads
    own, rest, far = level_weights(depth, lax.axis_index("seq"), index[:, lo : lo + rows], table)
    raw_q = late_sum(base, pieces, q_weight, q_early, lo, rows)
    causal = lax.broadcasted_iota(jnp.int32, (rows, rows), 0) >= lax.broadcasted_iota(jnp.int32, (rows, rows), 1)
    for head in range(heads):
        cols = slice(head * size, (head + 1) * size)
        query = unit_rows(raw_q[:, cols])
        scores = dot(query, keys[:, cols], ((1,), (1,)))
        scores = jnp.where(causal, scores, 0.0).astype(BF16)
        local = dot(scores, values[:, cols])
        if lo:
            local = local + dot(query, state_in[head].astype(BF16))
        wide = query.astype(F32)
        empty = (wide * rest[:, cols]).astype(BF16)
        part[:, cols] = own[:, cols] * local + dot(empty, jnp.zeros((size, size), BF16))
        for level in range(depth):
            scaled[level][:, cols] = (wide * far[level][:, cols]).astype(BF16)


def add_kernel(total, partner, grown, low):
    summed = total[...] + partner[...].astype(F32)
    grown[...] = summed
    low[...] = summed.astype(BF16)


def final_kernel(heads, depth, edges, *refs):
    count = len(edges) - 1
    parts = refs[:count]
    scaled = [refs[count * (1 + level) : count * (2 + level)] for level in range(depth)]
    refs = refs[count * (1 + depth) :]
    merged = refs[:depth]
    gain, out, done, sems = refs[depth:]
    size = done.shape[1] // heads
    copies = []
    for i in range(count):
        rows = slice(edges[i], edges[i + 1])
        for head in range(heads):
            cols = slice(head * size, (head + 1) * size)
            total = parts[i][:, cols]
            for level in range(depth):
                total = total + dot(scaled[level][i][:, cols], merged[level][head])
            total = total * lax.rsqrt(jnp.mean(total * total, -1, keepdims=True) + EPS)
            done[rows, cols] = (total * gain[0:1, cols]).astype(BF16)
        copy = pltpu.make_async_copy(done.at[rows], out.at[rows], sems.at[i])
        copy.start()
        copies.append(copy)
    for copy in copies:
        copy.wait()


def hop(piece, base):
    pieces = [piece]
    apart = 1
    while apart < base:
        pieces += [swap(piece, "head", apart) for piece in pieces]
        apart *= 2
    return pieces


def on_device(tokens, q_weight, k_weight, v_weight, level_table, level_index, out_gain):
    row_count, feat_here = tokens.shape
    width = q_weight.shape[1]
    heads, quant = level_table.shape
    size = width // heads
    base = lax.axis_size("head") // 2
    depth = lax.axis_size("seq").bit_length() - 1

    unit = row_count // sum(CHUNKS)
    edges = [0]
    for share in CHUNKS:
        edges.append(edges[-1] + share * unit)
    spans = list(zip(edges[:-1], edges[1:]))

    q_weight, k_weight, v_weight = (keep(weight) for weight in (q_weight, k_weight, v_weight))

    cuts = []
    for group in (spans[:1], spans[1:]):
        cuts += call(
            functools.partial(cut_kernel, group),
            [((hi - lo, feat_here), BF16) for lo, hi in group],
            [ANY],
            (tokens,),
            scratch=[pltpu.SemaphoreType.DMA((len(group),))],
        )
    far = [swap(piece, "head", base) for piece in cuts]
    near = hop(tokens, base)

    big = (row_count, width)
    early = call(
        functools.partial(early_kernel, base, row_count // 4),
        [(big, F32)] * 3,
        [VMEM] * (base + 3),
        (*near, q_weight, k_weight, v_weight),
    )
    table = call(table_kernel, [((2 * quant, width), BF16)], [VMEM], (level_table,))[0]

    state = []
    parts = []
    scaled = []
    for i, (lo, hi) in enumerate(spans):
        rows = hi - lo
        pieces = hop(far[i], base)
        before = state
        args = (*pieces, k_weight, v_weight, early[1], early[2], *before)
        keys, values, total, low = call(
            functools.partial(kv_kernel, base, lo, heads),
            [((rows, width), BF16)] * 2 + [((heads, size, size), F32), ((heads, size, size), BF16)],
            [VMEM] * len(args),
            args,
        )
        state = [total]
        args = (*pieces, q_weight, early[0], keys, values, level_index, table, *before)
        outs = call(
            functools.partial(query_kernel, base, lo, heads, depth),
            [((rows, width), F32)] + [((rows, width), BF16)] * depth,
            [VMEM] * len(args),
            args,
        )
        parts.append(outs[0])
        scaled.append(outs[1:])

    merged = []
    for level in range(depth):
        partner = swap(low, "seq", 1 << level)
        merged.append(partner)
        if level + 1 < depth:
            shape = (heads, size, size)
            total, low = call(add_kernel, [(shape, F32), (shape, BF16)], [VMEM, VMEM], (total, partner))

    inputs = parts + [chunk[level] for level in range(depth) for chunk in scaled] + merged
    return call(
        functools.partial(final_kernel, heads, depth, edges),
        [(big, BF16)],
        [VMEM] * (len(inputs) + 1),
        (*inputs, out_gain.reshape(1, width)),
        out_specs=[ANY],
        scratch=[pltpu.VMEM(big, BF16), pltpu.SemaphoreType.DMA((len(spans),))],
    )[0]


def solution(mesh):
    return jax.shard_map(
        on_device,
        mesh=mesh,
        in_specs=(
            P(("groups", "seq"), "head"),
            P(None, "head"),
            P(None, "head"),
            P(None, "head"),
            P("head", None),
            P(None, ("groups", "seq")),
            P("head"),
        ),
        out_specs=P(("groups", "seq"), "head"),
        check_vma=False,
    )
```

```python
import functools

import jax
import jax.numpy as jnp
from jax import lax
from jax.experimental import pallas as pl
from jax.experimental.pallas import tpu as pltpu
from jax.sharding import PartitionSpec as P


CHUNKS = (3, 2, 2, 1)
EPS = 1e-06
F32 = jnp.float32
BF16 = jnp.bfloat16
VMEM = pl.BlockSpec(memory_space=pltpu.VMEM)
ANY = pl.BlockSpec(memory_space=pl.ANY)
HBM = pl.BlockSpec(memory_space=pltpu.HBM)


def swap(block, axis, apart):
    route = [(i, i ^ apart) for i in range(lax.axis_size(axis))]
    return lax.ppermute(block, axis, route)


def dot(a, b, dims=((1,), (0,))):
    return lax.dot_general(a, b, (dims, ((), ())), preferred_element_type=F32)


def outside(array):
    return pltpu.with_memory_space_constraint(array, pltpu.HBM)


def call(kernel, outs, in_specs, args, out_specs=None, scratch=(), limit=8):
    kept = [pltpu.VMEM(*out) for out in outs]
    return pl.pallas_call(
        kernel,
        out_shape=kept if out_specs is None else [jax.ShapeDtypeStruct(*out) for out in outs],
        in_specs=in_specs,
        out_specs=out_specs or [VMEM] * len(outs),
        scratch_shapes=scratch,
        compiler_params=pltpu.CompilerParams(vmem_limit_bytes=limit << 20),
    )(*args)


def weight_rows(me, weight, offset, depth):
    start = pl.multiple_of((me ^ offset) * depth, depth)
    return weight[pl.ds(start, depth), :]


def unit_rows(raw):
    return (raw * lax.rsqrt(jnp.sum(raw * raw, -1, keepdims=True) + EPS)).astype(BF16)


def cut_kernel(spans, tokens, *refs):
    count = len(spans)
    outs, sems = refs[:count], refs[count]
    copies = []
    for i, (lo, hi) in enumerate(spans):
        copy = pltpu.make_async_copy(tokens.at[lo:hi], outs[i], sems.at[i])
        copy.start()
        copies.append(copy)
    for copy in copies:
        copy.wait()


def own_kernel(n_head, tokens, *refs):
    me = lax.axis_index("head")
    sources, weights, sums = refs[:3], refs[3:6], refs[6:9]
    held, held_sem, sems = refs[9:]
    depth = tokens.shape[1]
    fetch = pltpu.make_async_copy(tokens, held, held_sem)
    fetch.start()

    def copies(offset):
        start = pl.multiple_of((me ^ offset) * depth, depth)
        at = pl.ds(start, depth)
        return [
            pltpu.make_async_copy(source.at[at], weight.at[at], sems.at[offset, i])
            for i, (source, weight) in enumerate(zip(sources, weights))
        ]

    loads = [copies(offset) for offset in range(n_head)]
    for load in loads:
        for copy in load:
            copy.start()
    fetch.wait()
    for copy, weight, total in zip(loads[0], weights, sums):
        copy.wait()
        total[...] = dot(held[...], weight_rows(me, weight, 0, depth))
    for load in loads[1:]:
        for copy in load:
            copy.wait()


def near_kernel(n_near, *refs):
    me = lax.axis_index("head")
    pieces, weights, before, sums = refs[:n_near], refs[n_near : n_near + 3], refs[n_near + 3 : n_near + 6], refs[n_near + 6 :]
    depth = pieces[0].shape[1]
    for weight, total, grown in zip(weights, before, sums):
        acc = total[...]
        for i, piece in enumerate(pieces):
            acc = acc + dot(piece[...], weight_rows(me, weight, 1 + i, depth))
        grown[...] = acc


def late_sum(base, pieces, weight, early, lo, rows):
    me = lax.axis_index("head")
    depth = pieces[0].shape[1]
    acc = early[lo : lo + rows, :]
    for offset, piece in enumerate(pieces):
        acc = acc + dot(piece[...], weight_rows(me, weight, base + offset, depth))
    return acc


def kv_kernel(base, lo, heads, *refs):
    pieces = refs[:base]
    k_weight, v_weight, k_early, v_early = refs[base : base + 4]
    state_in = refs[base + 4] if lo else None
    keys, values, state, state_low = refs[-4:]
    rows, width = keys.shape
    size = width // heads
    raw_k = late_sum(base, pieces, k_weight, k_early, lo, rows)
    raw_v = late_sum(base, pieces, v_weight, v_early, lo, rows).astype(BF16)
    values[...] = raw_v
    for head in range(heads):
        cols = slice(head * size, (head + 1) * size)
        key = unit_rows(raw_k[:, cols])
        keys[:, cols] = key
        total = dot(key, raw_v[:, cols], ((0,), (0,)))
        if lo:
            total = state_in[head] + total
        state[head] = total
        state_low[head] = total.astype(BF16)


def table_kernel(table, wide):
    heads, _ = table.shape
    width = wide.shape[1]
    size = width // heads
    row = lax.broadcasted_iota(jnp.int32, (heads, width), 0)
    col = lax.broadcasted_iota(jnp.int32, (heads, width), 1)
    mine = ((col >= row * size) & (col < (row + 1) * size)).astype(BF16)
    exact = table[...]
    high = exact.astype(BF16)
    low = (exact - high.astype(F32)).astype(BF16)
    both = [dot(part, mine, ((0,), (0,))).astype(BF16) for part in (high, low)]
    wide[...] = jnp.concatenate(both, 0)


def level_weights(depth, block, index, table):
    quant = table.shape[0] // 2
    levels, rows = index.shape
    spot = lax.broadcasted_iota(jnp.int32, (quant, rows), 0)

    def picked(level):
        return (index[level : level + 1, :] == spot).astype(F32)

    def weigh(hot):
        hot = hot.astype(BF16)
        return dot(jnp.concatenate([hot, hot], 0), table[...], ((0,), (0,)))

    rest = jnp.zeros((quant, rows), F32)
    for level in range(depth + 1, levels):
        rest = rest + picked(level)
    far = [weigh(picked(level + 1)) * (block >> level & 1).astype(F32) for level in range(depth)]
    return weigh(picked(0)), weigh(rest), far


def query_kernel(base, lo, heads, depth, *refs):
    pieces = refs[:base]
    q_weight, q_early, keys, values, index, table = refs[base : base + 6]
    state_in = refs[base + 6] if lo else None
    part = refs[-1 - depth]
    scaled = refs[-depth:]
    rows, width = keys.shape
    size = width // heads
    own, rest, far = level_weights(depth, lax.axis_index("seq"), index[:, lo : lo + rows], table)
    raw_q = late_sum(base, pieces, q_weight, q_early, lo, rows)
    causal = lax.broadcasted_iota(jnp.int32, (rows, rows), 0) >= lax.broadcasted_iota(jnp.int32, (rows, rows), 1)
    for head in range(heads):
        cols = slice(head * size, (head + 1) * size)
        query = unit_rows(raw_q[:, cols])
        scores = dot(query, keys[:, cols], ((1,), (1,)))
        scores = jnp.where(causal, scores, 0.0).astype(BF16)
        local = dot(scores, values[:, cols])
        if lo:
            local = local + dot(query, state_in[head].astype(BF16))
        wide = query.astype(F32)
        empty = (wide * rest[:, cols]).astype(BF16)
        part[:, cols] = own[:, cols] * local + dot(empty, jnp.zeros((size, size), BF16))
        for level in range(depth):
            scaled[level][:, cols] = (wide * far[level][:, cols]).astype(BF16)


def add_kernel(total, partner, *grown):
    summed = total[...] + partner[...].astype(F32)
    for out in grown:
        out[...] = summed.astype(out.dtype)


def final_kernel(heads, depth, edges, *refs):
    count = len(edges) - 1
    parts = refs[:count]
    scaled = [refs[count * (1 + level) : count * (2 + level)] for level in range(depth)]
    refs = refs[count * (1 + depth) :]
    merged = refs[:depth]
    gain, out, done, sems = refs[depth:]
    size = done.shape[1] // heads
    copies = []
    for i in range(count):
        rows = slice(edges[i], edges[i + 1])
        for head in range(heads):
            cols = slice(head * size, (head + 1) * size)
            total = parts[i][:, cols]
            for level in range(depth):
                total = total + dot(scaled[level][i][:, cols], merged[level][head])
            total = total * lax.rsqrt(jnp.mean(total * total, -1, keepdims=True) + EPS)
            done[rows, cols] = (total * gain[0:1, cols]).astype(BF16)
        copy = pltpu.make_async_copy(done.at[rows], out.at[rows], sems.at[i])
        copy.start()
        copies.append(copy)
    for copy in copies:
        copy.wait()


def hop(piece, base):
    pieces = [piece]
    apart = 1
    while apart < base:
        pieces += [swap(piece, "head", apart) for piece in pieces]
        apart *= 2
    return pieces


def on_device(tokens, q_weight, k_weight, v_weight, level_table, level_index, out_gain):
    row_count, feat_here = tokens.shape
    width = q_weight.shape[1]
    heads, quant = level_table.shape
    size = width // heads
    base = lax.axis_size("head") // 2
    depth = lax.axis_size("seq").bit_length() - 1

    unit = row_count // sum(CHUNKS)
    edges = [0]
    for share in CHUNKS:
        edges.append(edges[-1] + share * unit)
    spans = list(zip(edges[:-1], edges[1:]))
    last = len(spans) - 1

    cuts = [tokens[: spans[0][1]]]
    cuts += call(
        functools.partial(cut_kernel, spans[1:]),
        [((hi - lo, feat_here), BF16) for lo, hi in spans[1:]],
        [HBM],
        (outside(tokens),),
        scratch=[pltpu.SemaphoreType.DMA((last,))],
    )
    far = [swap(piece, "head", base) for piece in cuts]
    near = hop(tokens, base)[1:]

    big = (row_count, width)
    *weights, q_own, k_own, v_own = call(
        functools.partial(own_kernel, 2 * base),
        [(q_weight.shape, BF16)] * 3 + [(big, F32)] * 3,
        [HBM] * 4,
        tuple(outside(array) for array in (tokens, q_weight, k_weight, v_weight)),
        scratch=[pltpu.VMEM(tokens.shape, BF16), pltpu.SemaphoreType.DMA, pltpu.SemaphoreType.DMA((2 * base, 3))],
    )
    q_weight, k_weight, v_weight = weights
    early = call(
        functools.partial(near_kernel, base - 1),
        [(big, F32)] * 3,
        [VMEM] * (base + 5),
        (*near, *weights, q_own, k_own, v_own),
    )
    table = call(table_kernel, [((2 * quant, width), BF16)], [VMEM], (level_table,))[0]

    state = []
    parts = []
    scaled = []
    for i, (lo, hi) in enumerate(spans):
        rows = hi - lo
        pieces = hop(far[i], base)
        before = state
        args = (*pieces, k_weight, v_weight, early[1], early[2], *before)
        keys, values, total, low = call(
            functools.partial(kv_kernel, base, lo, heads),
            [((rows, width), BF16)] * 2 + [((heads, size, size), F32), ((heads, size, size), BF16)],
            [VMEM] * len(args),
            args,
        )
        state = [total]
        args = (*pieces, q_weight, early[0], keys, values, level_index, table, *before)
        outs = call(
            functools.partial(query_kernel, base, lo, heads, depth),
            [((rows, width), F32)] + [((rows, width), BF16)] * depth,
            [VMEM] * len(args),
            args,
        )
        parts.append(outs[0])
        scaled.append(outs[1:])

    merged = []
    for level in range(depth):
        partner = swap(low, "seq", 1 << level)
        merged.append(partner)
        if level + 1 < depth:
            shape = (heads, size, size)
            kinds = [(shape, BF16)] + [(shape, F32)] * (level + 2 < depth)
            low, *rest = call(add_kernel, kinds, [VMEM, VMEM], (total, partner))
            total = rest[0] if rest else None

    inputs = parts + [chunk[level] for level in range(depth) for chunk in scaled] + merged
    return call(
        functools.partial(final_kernel, heads, depth, edges),
        [(big, BF16)],
        [VMEM] * (len(inputs) + 1),
        (*inputs, out_gain.reshape(1, width)),
        out_specs=[ANY],
        scratch=[pltpu.VMEM(big, BF16), pltpu.SemaphoreType.DMA((len(spans),))],
    )[0]


def solution(mesh):
    return jax.shard_map(
        on_device,
        mesh=mesh,
        in_specs=(
            P(("groups", "seq"), "head"),
            P(None, "head"),
            P(None, "head"),
            P(None, "head"),
            P("head", None),
            P(None, ("groups", "seq")),
            P("head"),
        ),
        out_specs=P(("groups", "seq"), "head"),
        check_vma=False,
    )
```

```python
import functools

import jax
import jax.numpy as jnp
from jax import lax
from jax.experimental import pallas as pl
from jax.experimental.pallas import tpu as pltpu
from jax.sharding import PartitionSpec as P


CHUNKS = (1, 5, 5, 3, 2)
EPS = 1e-06
F32 = jnp.float32
BF16 = jnp.bfloat16
VMEM = pl.BlockSpec(memory_space=pltpu.VMEM)
ANY = pl.BlockSpec(memory_space=pl.ANY)
HBM = pl.BlockSpec(memory_space=pltpu.HBM)


def swap(block, axis, apart):
    route = [(i, i ^ apart) for i in range(lax.axis_size(axis))]
    return lax.ppermute(block, axis, route)


def dot(a, b, dims=((1,), (0,))):
    return lax.dot_general(a, b, (dims, ((), ())), preferred_element_type=F32)


def outside(array):
    return pltpu.with_memory_space_constraint(array, pltpu.HBM)


def call(kernel, outs, in_specs, args, out_specs=None, scratch=(), limit=8):
    kept = [pltpu.VMEM(*out) for out in outs]
    return pl.pallas_call(
        kernel,
        out_shape=kept if out_specs is None else [jax.ShapeDtypeStruct(*out) for out in outs],
        in_specs=in_specs,
        out_specs=out_specs or [VMEM] * len(outs),
        scratch_shapes=scratch,
        compiler_params=pltpu.CompilerParams(vmem_limit_bytes=limit << 20),
    )(*args)


def weight_rows(me, weight, offset, depth):
    start = pl.multiple_of((me ^ offset) * depth, depth)
    return weight[pl.ds(start, depth), :]


def unit_rows(raw):
    return (raw * lax.rsqrt(jnp.sum(raw * raw, -1, keepdims=True) + EPS)).astype(BF16)


def cut_kernel(boxes, tokens, *refs):
    count = len(boxes)
    outs, sems = refs[:count], refs[count]
    copies = []
    for i, (lo, hi, wide) in enumerate(boxes):
        copy = pltpu.make_async_copy(tokens.at[lo:hi, :wide], outs[i], sems.at[i])
        copy.start()
        copies.append(copy)
    for copy in copies:
        copy.wait()


def own_kernel(n_head, tokens, *refs):
    me = lax.axis_index("head")
    sources, weights, sums = refs[:3], refs[3:6], refs[6:9]
    held, held_sem, sems = refs[9:]
    depth = tokens.shape[1]
    fetch = pltpu.make_async_copy(tokens, held, held_sem)
    fetch.start()

    def copies(offset):
        start = pl.multiple_of((me ^ offset) * depth, depth)
        at = pl.ds(start, depth)
        return [
            pltpu.make_async_copy(source.at[at], weight.at[at], sems.at[offset, i])
            for i, (source, weight) in enumerate(zip(sources, weights))
        ]

    loads = [copies(offset) for offset in range(n_head)]
    for load in loads:
        for copy in load:
            copy.start()
    fetch.wait()
    for copy, weight, total in zip(loads[0], weights, sums):
        copy.wait()
        total[...] = dot(held[...], weight_rows(me, weight, 0, depth))
    for load in loads[1:]:
        for copy in load:
            copy.wait()


def near_kernel(n_near, *refs):
    me = lax.axis_index("head")
    pieces, weights, before, sums = refs[:n_near], refs[n_near : n_near + 3], refs[n_near + 3 : n_near + 6], refs[n_near + 6 :]
    depth = pieces[0].shape[1]
    for weight, total, grown in zip(weights, before, sums):
        acc = total[...]
        for i, piece in enumerate(pieces):
            acc = acc + dot(piece[...], weight_rows(me, weight, 1 + i, depth))
        grown[...] = acc


def late_sum(base, pieces, weight, early, lo, rows):
    me = lax.axis_index("head")
    depth = pieces[0].shape[1]
    acc = early[lo : lo + rows, :]
    for offset, piece in enumerate(pieces):
        acc = acc + dot(piece[...], weight_rows(me, weight, base + offset, depth))
    return acc


def kv_kernel(base, lo, heads, *refs):
    pieces = refs[:base]
    k_weight, v_weight, k_early, v_early = refs[base : base + 4]
    state_in = refs[base + 4] if lo else None
    keys, values, state, state_low = refs[-4:]
    rows, width = keys.shape
    size = width // heads
    raw_k = late_sum(base, pieces, k_weight, k_early, lo, rows)
    raw_v = late_sum(base, pieces, v_weight, v_early, lo, rows).astype(BF16)
    values[...] = raw_v
    for head in range(heads):
        cols = slice(head * size, (head + 1) * size)
        key = unit_rows(raw_k[:, cols])
        keys[:, cols] = key
        total = dot(key, raw_v[:, cols], ((0,), (0,)))
        if lo:
            total = state_in[head] + total
        state[head] = total
        state_low[head] = total.astype(BF16)


def table_kernel(table, wide):
    heads, _ = table.shape
    width = wide.shape[1]
    size = width // heads
    row = lax.broadcasted_iota(jnp.int32, (heads, width), 0)
    col = lax.broadcasted_iota(jnp.int32, (heads, width), 1)
    mine = ((col >= row * size) & (col < (row + 1) * size)).astype(BF16)
    exact = table[...]
    high = exact.astype(BF16)
    low = (exact - high.astype(F32)).astype(BF16)
    both = [dot(part, mine, ((0,), (0,))).astype(BF16) for part in (high, low)]
    wide[...] = jnp.concatenate(both, 0)


def level_weights(depth, block, index, table):
    quant = table.shape[0] // 2
    levels, rows = index.shape
    spot = lax.broadcasted_iota(jnp.int32, (quant, rows), 0)

    def picked(level):
        return (index[level : level + 1, :] == spot).astype(F32)

    def weigh(hot):
        hot = hot.astype(BF16)
        return dot(jnp.concatenate([hot, hot], 0), table[...], ((0,), (0,)))

    rest = jnp.zeros((quant, rows), F32)
    for level in range(depth + 1, levels):
        rest = rest + picked(level)
    far = [weigh(picked(level + 1)) * (block >> level & 1).astype(F32) for level in range(depth)]
    return weigh(picked(0)), weigh(rest), far


def query_kernel(base, lo, heads, depth, *refs):
    pieces = refs[:base]
    q_weight, q_early, keys, values, index, table = refs[base : base + 6]
    state_in = refs[base + 6] if lo else None
    part = refs[-1 - depth]
    scaled = refs[-depth:]
    rows, width = keys.shape
    size = width // heads
    own, rest, far = level_weights(depth, lax.axis_index("seq"), index[:, lo : lo + rows], table)
    raw_q = late_sum(base, pieces, q_weight, q_early, lo, rows)
    causal = lax.broadcasted_iota(jnp.int32, (rows, rows), 0) >= lax.broadcasted_iota(jnp.int32, (rows, rows), 1)
    for head in range(heads):
        cols = slice(head * size, (head + 1) * size)
        query = unit_rows(raw_q[:, cols])
        scores = dot(query, keys[:, cols], ((1,), (1,)))
        scores = jnp.where(causal, scores, 0.0).astype(BF16)
        local = dot(scores, values[:, cols])
        if lo:
            local = local + dot(query, state_in[head].astype(BF16))
        wide = query.astype(F32)
        empty = (wide * rest[:, cols]).astype(BF16)
        part[:, cols] = own[:, cols] * local + dot(empty, jnp.zeros((size, size), BF16))
        for level in range(depth):
            scaled[level][:, cols] = (wide * far[level][:, cols]).astype(BF16)


def add_kernel(total, partner, *grown):
    summed = total[...] + partner[...].astype(F32)
    for out in grown:
        out[...] = summed.astype(out.dtype)


def fold_kernel(heads, levels, edges, *refs):
    count = len(edges) - 1
    parts = refs[:count]
    scaled = [refs[count * (1 + level) : count * (2 + level)] for level in range(levels)]
    merged = refs[count * (1 + levels) :][:levels]
    total = refs[-1]
    size = total.shape[1] // heads
    for i in range(count):
        rows = slice(edges[i], edges[i + 1])
        for head in range(heads):
            cols = slice(head * size, (head + 1) * size)
            acc = parts[i][:, cols]
            for level in range(levels):
                acc = acc + dot(scaled[level][i][:, cols], merged[level][head])
            total[rows, cols] = acc


def final_kernel(heads, edges, *refs):
    count = len(edges) - 1
    scaled = refs[:count]
    before, merged, gain, out, done, sems = refs[count:]
    size = done.shape[1] // heads
    share = jnp.full((size, size), 1.0 / size, BF16)
    copies = []
    for i in range(count):
        rows = slice(edges[i], edges[i + 1])
        for head in range(heads):
            cols = slice(head * size, (head + 1) * size)
            total = before[rows, cols] + dot(scaled[i][:, cols], merged[head])
            mean = dot((total * total).astype(BF16), share)
            done[rows, cols] = (total * lax.rsqrt(mean + EPS) * gain[0:1, cols]).astype(BF16)
        copy = pltpu.make_async_copy(done.at[rows], out.at[rows], sems.at[i])
        copy.start()
        copies.append(copy)
    for copy in copies:
        copy.wait()


def hop(piece, base):
    pieces = [piece]
    apart = 1
    while apart < base:
        pieces += [swap(piece, "head", apart) for piece in pieces]
        apart *= 2
    return pieces


def on_device(tokens, q_weight, k_weight, v_weight, level_table, level_index, out_gain):
    row_count, feat_here = tokens.shape
    width = q_weight.shape[1]
    heads, quant = level_table.shape
    size = width // heads
    base = lax.axis_size("head") // 2
    depth = lax.axis_size("seq").bit_length() - 1

    unit = row_count // sum(CHUNKS)
    edges = [0]
    for share in CHUNKS:
        edges.append(edges[-1] + share * unit)
    spans = list(zip(edges[:-1], edges[1:]))

    cuts = [tokens[: spans[0][1]]]
    boxes = [(lo, hi, feat_here) for lo, hi in spans[1:]] + [(0, 16, 128)]
    *rest, small = call(
        functools.partial(cut_kernel, boxes),
        [((hi - lo, wide), BF16) for lo, hi, wide in boxes],
        [HBM],
        (outside(tokens),),
        scratch=[pltpu.SemaphoreType.DMA((len(boxes),))],
    )
    cuts += rest
    greetings = [swap(small, "seq", 1 << level) for level in range(depth)]
    far = [swap(piece, "head", base) for piece in cuts]
    near = hop(tokens, base)[1:]

    big = (row_count, width)
    *weights, q_own, k_own, v_own = call(
        functools.partial(own_kernel, 2 * base),
        [(q_weight.shape, BF16)] * 3 + [(big, F32)] * 3,
        [HBM] * 4,
        tuple(outside(array) for array in (tokens, q_weight, k_weight, v_weight)),
        scratch=[pltpu.VMEM(tokens.shape, BF16), pltpu.SemaphoreType.DMA, pltpu.SemaphoreType.DMA((2 * base, 3))],
    )
    q_weight, k_weight, v_weight = weights
    early = call(
        functools.partial(near_kernel, base - 1),
        [(big, F32)] * 3,
        [VMEM] * (base + 5),
        (*near, *weights, q_own, k_own, v_own),
    )
    table = call(table_kernel, [((2 * quant, width), BF16)], [VMEM], (level_table,))[0]

    state = []
    parts = []
    scaled = []
    for i, (lo, hi) in enumerate(spans):
        rows = hi - lo
        pieces = hop(far[i], base)
        before = state
        args = (*pieces, k_weight, v_weight, early[1], early[2], *before)
        keys, values, total, low = call(
            functools.partial(kv_kernel, base, lo, heads),
            [((rows, width), BF16)] * 2 + [((heads, size, size), F32), ((heads, size, size), BF16)],
            [VMEM] * len(args),
            args,
        )
        state = [total]
        args = (*pieces, q_weight, early[0], keys, values, level_index, table, *before)
        outs = call(
            functools.partial(query_kernel, base, lo, heads, depth),
            [((rows, width), F32)] + [((rows, width), BF16)] * depth,
            [VMEM] * len(args),
            args,
        )
        parts.append(outs[0])
        scaled.append(outs[1:])

    merged = []
    for level in range(depth):
        partner = swap(low, "seq", 1 << level)
        merged.append(partner)
        if level + 1 < depth:
            shape = (heads, size, size)
            kinds = [(shape, BF16)] + [(shape, F32)] * (level + 2 < depth)
            low, *rest = call(add_kernel, kinds, [VMEM, VMEM], (total, partner))
            total = rest[0] if rest else None

    inputs = parts + [chunk[level] for level in range(depth - 1) for chunk in scaled] + merged[:-1] + greetings
    before = call(
        functools.partial(fold_kernel, heads, depth - 1, edges), [(big, F32)], [VMEM] * len(inputs), inputs
    )[0]
    inputs = [chunk[-1] for chunk in scaled] + [before, merged[-1], out_gain.reshape(1, width)]
    return call(
        functools.partial(final_kernel, heads, edges),
        [(big, BF16)],
        [VMEM] * len(inputs),
        inputs,
        out_specs=[ANY],
        scratch=[pltpu.VMEM(big, BF16), pltpu.SemaphoreType.DMA((len(spans),))],
    )[0]


def solution(mesh):
    return jax.shard_map(
        on_device,
        mesh=mesh,
        in_specs=(
            P(("groups", "seq"), "head"),
            P(None, "head"),
            P(None, "head"),
            P(None, "head"),
            P("head", None),
            P(None, ("groups", "seq")),
            P("head"),
        ),
        out_specs=P(("groups", "seq"), "head"),
        check_vma=False,
    )
```

```python
import functools

import jax
import jax.numpy as jnp
from jax import lax
from jax.experimental import pallas as pl
from jax.experimental.pallas import tpu as pltpu
from jax.sharding import PartitionSpec as P


CHUNKS = (3, 2, 2, 1)
EPS = 1e-06
F32 = jnp.float32
BF16 = jnp.bfloat16
VMEM = pl.BlockSpec(memory_space=pltpu.VMEM)
ANY = pl.BlockSpec(memory_space=pl.ANY)
HBM = pl.BlockSpec(memory_space=pltpu.HBM)


def swap(block, axis, apart):
    route = [(i, i ^ apart) for i in range(lax.axis_size(axis))]
    return lax.ppermute(block, axis, route)


def dot(a, b, dims=((1,), (0,))):
    return lax.dot_general(a, b, (dims, ((), ())), preferred_element_type=F32)


def outside(array):
    return pltpu.with_memory_space_constraint(array, pltpu.HBM)


def call(kernel, outs, in_specs, args, out_specs=None, scratch=(), limit=8, aliases={}):
    kept = [pltpu.VMEM(*out) for out in outs]
    return pl.pallas_call(
        kernel,
        out_shape=kept if out_specs is None else [jax.ShapeDtypeStruct(*out) for out in outs],
        in_specs=in_specs,
        out_specs=out_specs or [VMEM] * len(outs),
        scratch_shapes=scratch,
        input_output_aliases=aliases,
        compiler_params=pltpu.CompilerParams(vmem_limit_bytes=limit << 20),
    )(*args)


def weight_rows(me, weight, offset, depth):
    start = pl.multiple_of((me ^ offset) * depth, depth)
    return weight[pl.ds(start, depth), :]


def unit_rows(raw):
    return (raw * lax.rsqrt(jnp.sum(raw * raw, -1, keepdims=True) + EPS)).astype(BF16)


def cut_kernel(boxes, tokens, *refs):
    count = len(boxes)
    outs, sems = refs[:count], refs[count]
    copies = []
    for i, (lo, hi, wide) in enumerate(boxes):
        copy = pltpu.make_async_copy(tokens.at[lo:hi, :wide], outs[i], sems.at[i])
        copy.start()
        copies.append(copy)
    for copy in copies:
        copy.wait()


def own_kernel(n_head, tokens, *refs):
    me = lax.axis_index("head")
    sources, weights, sums = refs[:3], refs[3:6], refs[6:9]
    held, held_sem, sems = refs[9:]
    depth = tokens.shape[1]
    fetch = pltpu.make_async_copy(tokens, held, held_sem)
    fetch.start()

    def copies(offset):
        start = pl.multiple_of((me ^ offset) * depth, depth)
        at = pl.ds(start, depth)
        return [
            pltpu.make_async_copy(source.at[at], weight.at[at], sems.at[offset, i])
            for i, (source, weight) in enumerate(zip(sources, weights))
        ]

    loads = [copies(offset) for offset in range(n_head)]
    for load in loads:
        for copy in load:
            copy.start()
    fetch.wait()
    for copy, weight, total in zip(loads[0], weights, sums):
        copy.wait()
        total[...] = dot(held[...], weight_rows(me, weight, 0, depth))
    for load in loads[1:]:
        for copy in load:
            copy.wait()


def near_kernel(n_near, *refs):
    me = lax.axis_index("head")
    pieces, weights, before, sums = refs[:n_near], refs[n_near : n_near + 3], refs[n_near + 3 : n_near + 6], refs[n_near + 6 :]
    depth = pieces[0].shape[1]
    for weight, total, grown in zip(weights, before, sums):
        acc = total[...]
        for i, piece in enumerate(pieces):
            acc = acc + dot(piece[...], weight_rows(me, weight, 1 + i, depth))
        grown[...] = acc


def late_sum(base, pieces, weight, early, lo, rows, cols):
    me = lax.axis_index("head")
    depth = pieces[0].shape[1]
    acc = early[lo : lo + rows, cols]
    for offset, piece in enumerate(pieces):
        start = pl.multiple_of((me ^ (base + offset)) * depth, depth)
        acc = acc + dot(piece[...], weight[pl.ds(start, depth), cols])
    return acc


def kv_kernel(base, lo, size, first, *refs):
    pieces = refs[:base]
    k_weight, v_weight, k_early, v_early = refs[base : base + 4]
    state_in = refs[base + 4 : -4]
    keys, values, state, state_low = refs[-4:]
    rows, width = keys.shape
    mine = slice(first * size, first * size + width)
    raw_k = late_sum(base, pieces, k_weight, k_early, lo, rows, mine)
    raw_v = late_sum(base, pieces, v_weight, v_early, lo, rows, mine).astype(BF16)
    values[...] = raw_v
    for head in range(width // size):
        cols = slice(head * size, (head + 1) * size)
        key = unit_rows(raw_k[:, cols])
        keys[:, cols] = key
        total = dot(key, raw_v[:, cols], ((0,), (0,)))
        if state_in:
            total = state_in[0][first + head] + total
        state[head] = total
        state_low[head] = total.astype(BF16)


def table_kernel(table, wide):
    heads, _ = table.shape
    width = wide.shape[1]
    size = width // heads
    row = lax.broadcasted_iota(jnp.int32, (heads, width), 0)
    col = lax.broadcasted_iota(jnp.int32, (heads, width), 1)
    mine = ((col >= row * size) & (col < (row + 1) * size)).astype(BF16)
    exact = table[...]
    high = exact.astype(BF16)
    low = (exact - high.astype(F32)).astype(BF16)
    both = [dot(part, mine, ((0,), (0,))).astype(BF16) for part in (high, low)]
    wide[...] = jnp.concatenate(both, 0)


def level_weights(depth, block, index, table):
    quant = table.shape[0] // 2
    levels, rows = index.shape
    spot = lax.broadcasted_iota(jnp.int32, (quant, rows), 0)

    def picked(level):
        return (index[level : level + 1, :] == spot).astype(F32)

    def weigh(hot):
        hot = hot.astype(BF16)
        return dot(jnp.concatenate([hot, hot], 0), table[...], ((0,), (0,)))

    rest = jnp.zeros((quant, rows), F32)
    for level in range(depth + 1, levels):
        rest = rest + picked(level)
    far = [weigh(picked(level + 1)) * (block >> level & 1).astype(F32) for level in range(depth)]
    return weigh(picked(0)), weigh(rest), far


def query_kernel(base, groups, lo, heads, depth, *refs):
    pieces = refs[:base]
    q_weight, q_early, index, table = refs[base : base + 4]
    keys = refs[base + 4 : base + 4 + groups]
    values = refs[base + 4 + groups : base + 4 + 2 * groups]
    state_in = refs[base + 4 + 2 * groups : -1 - depth]
    part = refs[-1 - depth]
    scaled = refs[-depth:]
    rows, width = part.shape
    size = width // heads
    per = heads // groups
    own, rest, far = level_weights(depth, lax.axis_index("seq"), index[:, lo : lo + rows], table)
    raw_q = late_sum(base, pieces, q_weight, q_early, lo, rows, slice(0, width))
    causal = lax.broadcasted_iota(jnp.int32, (rows, rows), 0) >= lax.broadcasted_iota(jnp.int32, (rows, rows), 1)
    for head in range(heads):
        cols = slice(head * size, (head + 1) * size)
        query = unit_rows(raw_q[:, cols])
        inside = slice(head % per * size, (head % per + 1) * size)
        scores = dot(query, keys[head // per][:, inside], ((1,), (1,)))
        scores = jnp.where(causal, scores, 0.0).astype(BF16)
        local = dot(scores, values[head // per][:, inside])
        if state_in:
            local = local + dot(query, state_in[0][head].astype(BF16))
        wide = query.astype(F32)
        empty = (wide * rest[:, cols]).astype(BF16)
        part[:, cols] = own[:, cols] * local + dot(empty, jnp.zeros((size, size), BF16))
        for level in range(depth):
            scaled[level][:, cols] = (wide * far[level][:, cols]).astype(BF16)


def add_kernel(total, partner, *grown):
    summed = total[...] + partner[...].astype(F32)
    for out in grown:
        out[...] = summed.astype(out.dtype)


def fold_kernel(heads, groups, levels, edges, *refs):
    count = len(edges) - 1
    parts = refs[:count]
    scaled = [refs[count * (1 + level) : count * (2 + level)] for level in range(levels)]
    merged = refs[count * (1 + levels) : -1]
    total = refs[-1]
    size = total.shape[1] // heads
    per = heads // groups
    for i in range(count):
        rows = slice(edges[i], edges[i + 1])
        for head in range(heads):
            cols = slice(head * size, (head + 1) * size)
            acc = parts[i][:, cols]
            for level in range(levels):
                acc = acc + dot(scaled[level][i][:, cols], merged[level * groups + head // per][head % per])
            total[rows, cols] = acc


def final_kernel(edges, first, *refs):
    count = len(edges) - 1
    scaled = refs[:count]
    before, merged, gain = refs[count : count + 3]
    out, done, sems = refs[-3:]
    per, size, _ = merged.shape
    mine = slice(first * size, (first + per) * size)
    share = jnp.full((size, size), 1.0 / size, BF16)
    copies = []
    for i in range(count):
        rows = slice(edges[i], edges[i + 1])
        for head in range(per):
            cols = slice((first + head) * size, (first + head + 1) * size)
            total = before[rows, cols] + dot(scaled[i][:, cols], merged[head])
            mean = dot((total * total).astype(BF16), share)
            done[rows, head * size : (head + 1) * size] = (total * lax.rsqrt(mean + EPS) * gain[0:1, cols]).astype(BF16)
        copy = pltpu.make_async_copy(done.at[rows], out.at[rows, mine], sems.at[i])
        copy.start()
        copies.append(copy)
    for copy in copies:
        copy.wait()


def hop(piece, base):
    pieces = [piece]
    apart = 1
    while apart < base:
        pieces += [swap(piece, "head", apart) for piece in pieces]
        apart *= 2
    return pieces


def on_device(tokens, q_weight, k_weight, v_weight, level_table, level_index, out_gain):
    row_count, feat_here = tokens.shape
    width = q_weight.shape[1]
    heads, quant = level_table.shape
    size = width // heads
    base = lax.axis_size("head") // 2
    depth = lax.axis_size("seq").bit_length() - 1

    unit = row_count // sum(CHUNKS)
    edges = [0]
    for share in CHUNKS:
        edges.append(edges[-1] + share * unit)
    spans = list(zip(edges[:-1], edges[1:]))
    last = len(spans) - 1

    cuts = [tokens[: spans[0][1]]]
    boxes = [(lo, hi, feat_here) for lo, hi in spans[1:]]
    cuts += call(
        functools.partial(cut_kernel, boxes),
        [((hi - lo, wide), BF16) for lo, hi, wide in boxes],
        [HBM],
        (outside(tokens),),
        scratch=[pltpu.SemaphoreType.DMA((len(boxes),))],
    )
    far = [swap(piece, "head", base) for piece in cuts]
    near = hop(tokens, base)[1:]

    big = (row_count, width)
    *weights, q_own, k_own, v_own = call(
        functools.partial(own_kernel, 2 * base),
        [(q_weight.shape, BF16)] * 3 + [(big, F32)] * 3,
        [HBM] * 4,
        tuple(outside(array) for array in (tokens, q_weight, k_weight, v_weight)),
        scratch=[pltpu.VMEM(tokens.shape, BF16), pltpu.SemaphoreType.DMA, pltpu.SemaphoreType.DMA((2 * base, 3))],
    )
    q_weight, k_weight, v_weight = weights
    early = call(
        functools.partial(near_kernel, base - 1),
        [(big, F32)] * 3,
        [VMEM] * (base + 5),
        (*near, *weights, q_own, k_own, v_own),
    )
    table = call(table_kernel, [((2 * quant, width), BF16)], [VMEM], (level_table,))[0]

    split = 2 - heads % 2
    per = heads // split
    state = []
    parts = []
    scaled = []
    for i, (lo, hi) in enumerate(spans):
        rows = hi - lo
        pieces = hop(far[i], base)
        groups = split if i == last else 1
        keys, values, totals, lows = [], [], [], []
        for group in range(groups):
            count = heads // groups
            args = (*pieces, k_weight, v_weight, early[1], early[2], *state)
            results = call(
                functools.partial(kv_kernel, base, lo, size, group * count),
                [((rows, count * size), BF16)] * 2 + [((count, size, size), F32), ((count, size, size), BF16)],
                [VMEM] * len(args),
                args,
            )
            for items, result in zip((keys, values, totals, lows), results):
                items.append(result)
        args = (*pieces, q_weight, early[0], level_index, table, *keys, *values, *state)
        outs = call(
            functools.partial(query_kernel, base, groups, lo, heads, depth),
            [((rows, width), F32)] + [((rows, width), BF16)] * depth,
            [VMEM] * len(args),
            args,
        )
        parts.append(outs[0])
        scaled.append(outs[1:])
        state = totals

    merged = []
    for level in range(depth):
        partners = [swap(low, "seq", 1 << level) for low in lows]
        merged.append(partners)
        if level + 1 < depth:
            shape = (per, size, size)
            kinds = [(shape, BF16)] + [(shape, F32)] * (level + 2 < depth)
            grown = [
                call(add_kernel, kinds, [VMEM, VMEM], (total, partner))
                for total, partner in zip(totals, partners)
            ]
            lows = [pair[0] for pair in grown]
            totals = [pair[-1] for pair in grown]

    inputs = parts + [chunk[level] for level in range(depth - 1) for chunk in scaled]
    inputs += [partner for partners in merged[:-1] for partner in partners]
    before = call(
        functools.partial(fold_kernel, heads, split, depth - 1, edges), [(big, F32)], [VMEM] * len(inputs), inputs
    )[0]
    out = []
    for group in range(split):
        inputs = [chunk[-1] for chunk in scaled] + [before, merged[-1][group], out_gain.reshape(1, width)]
        out = list(call(
            functools.partial(final_kernel, edges, group * per),
            [(big, BF16)],
            [VMEM] * len(inputs) + [ANY] * len(out),
            inputs + out,
            out_specs=[ANY],
            scratch=[pltpu.VMEM((row_count, per * size), BF16), pltpu.SemaphoreType.DMA((len(spans),))],
            aliases={len(inputs): 0} if out else {},
        ))
    return out[0]


def solution(mesh):
    return jax.shard_map(
        on_device,
        mesh=mesh,
        in_specs=(
            P(("groups", "seq"), "head"),
            P(None, "head"),
            P(None, "head"),
            P(None, "head"),
            P("head", None),
            P(None, ("groups", "seq")),
            P("head"),
        ),
        out_specs=P(("groups", "seq"), "head"),
        check_vma=False,
    )
```

```python
import functools

import jax
import jax.numpy as jnp
from jax import lax
from jax.experimental import pallas as pl
from jax.experimental.pallas import tpu as pltpu
from jax.sharding import PartitionSpec as P


CHUNKS = (4, 5, 4, 3)
EPS = 1e-06
F32 = jnp.float32
BF16 = jnp.bfloat16
VMEM = pl.BlockSpec(memory_space=pltpu.VMEM)
ANY = pl.BlockSpec(memory_space=pl.ANY)
HBM = pl.BlockSpec(memory_space=pltpu.HBM)


def swap(block, axis, apart):
    route = [(i, i ^ apart) for i in range(lax.axis_size(axis))]
    return lax.ppermute(block, axis, route)


def dot(a, b, dims=((1,), (0,))):
    return lax.dot_general(a, b, (dims, ((), ())), preferred_element_type=F32)


def outside(array):
    return pltpu.with_memory_space_constraint(array, pltpu.HBM)


def call(kernel, outs, in_specs, args, out_specs=None, scratch=(), limit=8, aliases={}):
    kept = [pltpu.VMEM(*out) for out in outs]
    return pl.pallas_call(
        kernel,
        out_shape=kept if out_specs is None else [jax.ShapeDtypeStruct(*out) for out in outs],
        in_specs=in_specs,
        out_specs=out_specs or [VMEM] * len(outs),
        scratch_shapes=scratch,
        input_output_aliases=aliases,
        compiler_params=pltpu.CompilerParams(vmem_limit_bytes=limit << 20),
    )(*args)


def weight_rows(me, weight, offset, depth):
    start = pl.multiple_of((me ^ offset) * depth, depth)
    return weight[pl.ds(start, depth), :]


def unit_rows(raw):
    return (raw * lax.rsqrt(jnp.sum(raw * raw, -1, keepdims=True) + EPS)).astype(BF16)


def cut_kernel(boxes, tokens, *refs):
    count = len(boxes)
    outs, sems = refs[:count], refs[count]
    copies = []
    for i, (lo, hi, wide) in enumerate(boxes):
        copy = pltpu.make_async_copy(tokens.at[lo:hi, :wide], outs[i], sems.at[i])
        copy.start()
        copies.append(copy)
    for copy in copies:
        copy.wait()


def own_kernel(n_head, tokens, *refs):
    me = lax.axis_index("head")
    sources, weights, sums = refs[:3], refs[3:6], refs[6:9]
    held, held_sem, sems = refs[9:]
    depth = tokens.shape[1]
    fetch = pltpu.make_async_copy(tokens, held, held_sem)
    fetch.start()

    def copies(offset):
        start = pl.multiple_of((me ^ offset) * depth, depth)
        at = pl.ds(start, depth)
        return [
            pltpu.make_async_copy(source.at[at], weight.at[at], sems.at[offset, i])
            for i, (source, weight) in enumerate(zip(sources, weights))
        ]

    loads = [copies(offset) for offset in range(n_head)]
    for load in loads:
        for copy in load:
            copy.start()
    fetch.wait()
    for copy, weight, total in zip(loads[0], weights, sums):
        copy.wait()
        total[...] = dot(held[...], weight_rows(me, weight, 0, depth))
    for load in loads[1:]:
        for copy in load:
            copy.wait()


def near_kernel(n_near, *refs):
    me = lax.axis_index("head")
    pieces, weights, before, sums = refs[:n_near], refs[n_near : n_near + 3], refs[n_near + 3 : n_near + 6], refs[n_near + 6 :]
    depth = pieces[0].shape[1]
    for weight, total, grown in zip(weights, before, sums):
        acc = total[...]
        for i, piece in enumerate(pieces):
            acc = acc + dot(piece[...], weight_rows(me, weight, 1 + i, depth))
        grown[...] = acc


def late_sum(base, pieces, weight, early, lo, rows, cols):
    me = lax.axis_index("head")
    depth = pieces[0].shape[1]
    acc = early[lo : lo + rows, cols]
    for offset, piece in enumerate(pieces):
        start = pl.multiple_of((me ^ (base + offset)) * depth, depth)
        acc = acc + dot(piece[...], weight[pl.ds(start, depth), cols])
    return acc


def kv_kernel(base, lo, size, first, *refs):
    pieces = refs[:base]
    k_weight, v_weight, k_early, v_early = refs[base : base + 4]
    state_in = refs[base + 4 : -4]
    keys, values, state, state_low = refs[-4:]
    rows, width = keys.shape
    mine = slice(first * size, first * size + width)
    raw_k = late_sum(base, pieces, k_weight, k_early, lo, rows, mine)
    raw_v = late_sum(base, pieces, v_weight, v_early, lo, rows, mine).astype(BF16)
    values[...] = raw_v
    for head in range(width // size):
        cols = slice(head * size, (head + 1) * size)
        key = unit_rows(raw_k[:, cols])
        keys[:, cols] = key
        total = dot(key, raw_v[:, cols], ((0,), (0,)))
        if state_in:
            total = state_in[0][first + head] + total
        state[head] = total
        state_low[head] = total.astype(BF16)


def table_kernel(table, wide):
    heads, _ = table.shape
    width = wide.shape[1]
    size = width // heads
    row = lax.broadcasted_iota(jnp.int32, (heads, width), 0)
    col = lax.broadcasted_iota(jnp.int32, (heads, width), 1)
    mine = ((col >= row * size) & (col < (row + 1) * size)).astype(BF16)
    exact = table[...]
    high = exact.astype(BF16)
    low = (exact - high.astype(F32)).astype(BF16)
    both = [dot(part, mine, ((0,), (0,))).astype(BF16) for part in (high, low)]
    wide[...] = jnp.concatenate(both, 0)


def level_kernel(depth, index, table, *outs):
    block = lax.axis_index("seq")
    quant = table.shape[0] // 2
    levels, rows = index.shape
    spot = lax.broadcasted_iota(jnp.int32, (quant, rows), 0)

    def picked(level):
        return (index[level : level + 1, :] == spot).astype(F32)

    def weigh(hot):
        hot = hot.astype(BF16)
        return dot(jnp.concatenate([hot, hot], 0), table[...], ((0,), (0,)))

    rest = jnp.zeros((quant, rows), F32)
    for level in range(depth + 1, levels):
        rest = rest + picked(level)
    outs[0][...] = weigh(picked(0))
    outs[1][...] = weigh(rest)
    for level in range(depth):
        outs[2 + level][...] = weigh(picked(level + 1)) * (block >> level & 1).astype(F32)


def query_kernel(base, groups, lo, heads, depth, *refs):
    pieces = refs[:base]
    q_weight, q_early, own, rest = refs[base : base + 4]
    far = refs[base + 4 : base + 4 + depth]
    at = base + 4 + depth
    keys = refs[at : at + groups]
    values = refs[at + groups : at + 2 * groups]
    state_in = refs[at + 2 * groups : -1 - depth]
    part = refs[-1 - depth]
    scaled = refs[-depth:]
    rows, width = part.shape
    size = width // heads
    per = heads // groups
    mine = slice(lo, lo + rows)
    raw_q = late_sum(base, pieces, q_weight, q_early, lo, rows, slice(0, width))
    causal = lax.broadcasted_iota(jnp.int32, (rows, rows), 0) >= lax.broadcasted_iota(jnp.int32, (rows, rows), 1)
    for head in range(heads):
        cols = slice(head * size, (head + 1) * size)
        query = unit_rows(raw_q[:, cols])
        inside = slice(head % per * size, (head % per + 1) * size)
        scores = dot(query, keys[head // per][:, inside], ((1,), (1,)))
        scores = jnp.where(causal, scores, 0.0).astype(BF16)
        local = dot(scores, values[head // per][:, inside])
        if state_in:
            local = local + dot(query, state_in[0][head].astype(BF16))
        wide = query.astype(F32)
        empty = (wide * rest[mine, cols]).astype(BF16)
        part[:, cols] = own[mine, cols] * local + dot(empty, jnp.zeros((size, size), BF16))
        for level in range(depth):
            scaled[level][:, cols] = (wide * far[level][mine, cols]).astype(BF16)


def add_kernel(total, partner, *grown):
    summed = total[...] + partner[...].astype(F32)
    for out in grown:
        out[...] = summed.astype(out.dtype)


def fold_kernel(heads, groups, levels, edges, *refs):
    count = len(edges) - 1
    parts = refs[:count]
    scaled = [refs[count * (1 + level) : count * (2 + level)] for level in range(levels)]
    merged = refs[count * (1 + levels) : -3]
    gain_in, total, gain = refs[-3:]
    gain[...] = gain_in[...]
    size = total.shape[1] // heads
    per = heads // groups
    for i in range(count):
        rows = slice(edges[i], edges[i + 1])
        for head in range(heads):
            cols = slice(head * size, (head + 1) * size)
            acc = parts[i][:, cols]
            for level in range(levels):
                acc = acc + dot(scaled[level][i][:, cols], merged[level * groups + head // per][head % per])
            total[rows, cols] = acc


def finish(edges, first, scaled, before, merged, gain, store):
    per, size, _ = merged.shape
    share = jnp.full((size, size), 1.0 / size, BF16)
    for i in range(len(edges) - 1):
        rows = slice(edges[i], edges[i + 1])
        for head in range(per):
            cols = slice((first + head) * size, (first + head + 1) * size)
            total = before[rows, cols] + dot(scaled[i][:, cols], merged[head])
            mean = dot((total * total).astype(BF16), share)
            ready = (total * lax.rsqrt(mean + EPS) * gain[0:1, cols]).astype(BF16)
            store(i, rows, slice(head * size, (head + 1) * size), ready)


def group_kernel(edges, first, *refs):
    count = len(edges) - 1
    before, merged, gain, done = refs[count:]

    def store(i, rows, cols, ready):
        done[rows, cols] = ready

    finish(edges, first, refs[:count], before, merged, gain, store)


def final_kernel(edges, first, *refs):
    count = len(edges) - 1
    before, merged, gain = refs[count : count + 3]
    ready = refs[count + 3 : -4]
    out, done, sems, ready_sems = refs[-4:]
    per, size, _ = merged.shape
    copies = []
    for i, part in enumerate(ready):
        width = part.shape[1]
        copies.append(pltpu.make_async_copy(part, out.at[:, i * width : (i + 1) * width], ready_sems.at[i]))
        copies[-1].start()
    mine = slice(first * size, (first + per) * size)

    def store(i, rows, cols, value):
        done[rows, cols] = value
        if cols.stop == per * size:
            copy = pltpu.make_async_copy(done.at[rows], out.at[rows, mine], sems.at[i])
            copy.start()
            copies.append(copy)

    finish(edges, first, refs[:count], before, merged, gain, store)
    for copy in copies:
        copy.wait()


def hop(piece, base):
    pieces = [piece]
    apart = 1
    while apart < base:
        pieces += [swap(piece, "head", apart) for piece in pieces]
        apart *= 2
    return pieces


def on_device(tokens, q_weight, k_weight, v_weight, level_table, level_index, out_gain):
    row_count, feat_here = tokens.shape
    width = q_weight.shape[1]
    heads, quant = level_table.shape
    size = width // heads
    base = lax.axis_size("head") // 2
    depth = lax.axis_size("seq").bit_length() - 1

    unit = row_count // sum(CHUNKS)
    edges = [0]
    for share in CHUNKS:
        edges.append(edges[-1] + share * unit)
    spans = list(zip(edges[:-1], edges[1:]))
    last = len(spans) - 1

    cuts = [tokens[: spans[0][1]]]
    boxes = [(lo, hi, feat_here) for lo, hi in spans[1:]]
    cuts += call(
        functools.partial(cut_kernel, boxes),
        [((hi - lo, wide), BF16) for lo, hi, wide in boxes],
        [HBM],
        (outside(tokens),),
        scratch=[pltpu.SemaphoreType.DMA((len(boxes),))],
    )
    far = [swap(piece, "head", base) for piece in cuts]
    near = hop(tokens, base)[1:]

    big = (row_count, width)
    *weights, q_own, k_own, v_own = call(
        functools.partial(own_kernel, 2 * base),
        [(q_weight.shape, BF16)] * 3 + [(big, F32)] * 3,
        [HBM] * 4,
        tuple(outside(array) for array in (tokens, q_weight, k_weight, v_weight)),
        scratch=[pltpu.VMEM(tokens.shape, BF16), pltpu.SemaphoreType.DMA, pltpu.SemaphoreType.DMA((2 * base, 3))],
    )
    q_weight, k_weight, v_weight = weights
    early = call(
        functools.partial(near_kernel, base - 1),
        [(big, F32)] * 3,
        [VMEM] * (base + 5),
        (*near, *weights, q_own, k_own, v_own),
    )
    table = call(table_kernel, [((2 * quant, width), BF16)], [VMEM], (level_table,))[0]
    levels = call(functools.partial(level_kernel, depth), [(big, F32)] * (2 + depth), [VMEM] * 2, (level_index, table))

    split = 2 - heads % 2
    per = heads // split
    state = []
    parts = []
    scaled = []
    for i, (lo, hi) in enumerate(spans):
        rows = hi - lo
        pieces = hop(far[i], base)
        groups = split if i == last else 1
        keys, values, totals, lows = [], [], [], []
        for group in range(groups):
            count = heads // groups
            args = (*pieces, k_weight, v_weight, early[1], early[2], *state)
            results = call(
                functools.partial(kv_kernel, base, lo, size, group * count),
                [((rows, count * size), BF16)] * 2 + [((count, size, size), F32), ((count, size, size), BF16)],
                [VMEM] * len(args),
                args,
            )
            for items, result in zip((keys, values, totals, lows), results):
                items.append(result)
        args = (*pieces, q_weight, early[0], *levels, *keys, *values, *state)
        outs = call(
            functools.partial(query_kernel, base, groups, lo, heads, depth),
            [((rows, width), F32)] + [((rows, width), BF16)] * depth,
            [VMEM] * len(args),
            args,
        )
        parts.append(outs[0])
        scaled.append(outs[1:])
        state = totals

    merged = []
    for level in range(depth):
        partners = [swap(low, "seq", 1 << level) for low in lows]
        merged.append(partners)
        if level + 1 < depth:
            shape = (per, size, size)
            kinds = [(shape, BF16)] + [(shape, F32)] * (level + 2 < depth)
            grown = [
                call(add_kernel, kinds, [VMEM, VMEM], (total, partner))
                for total, partner in zip(totals, partners)
            ]
            lows = [pair[0] for pair in grown]
            totals = [pair[-1] for pair in grown]

    inputs = parts + [chunk[level] for level in range(depth - 1) for chunk in scaled]
    inputs += [partner for partners in merged[:-1] for partner in partners] + [out_gain.reshape(1, width)]
    before, gain = call(
        functools.partial(fold_kernel, heads, split, depth - 1, edges),
        [(big, F32), ((1, width), F32)],
        [VMEM] * len(inputs),
        inputs,
    )
    ready = []
    for group in range(split):
        inputs = [chunk[-1] for chunk in scaled] + [before, merged[-1][group], gain]
        if group + 1 < split:
            kind = ((row_count, per * size), BF16)
            kernel = functools.partial(group_kernel, edges, group * per)
            ready += call(kernel, [kind], [VMEM] * len(inputs), inputs)
    inputs += ready
    return call(
        functools.partial(final_kernel, edges, (split - 1) * per),
        [(big, BF16)],
        [VMEM] * len(inputs),
        inputs,
        out_specs=[ANY],
        scratch=[
            pltpu.VMEM((row_count, per * size), BF16),
            pltpu.SemaphoreType.DMA((len(spans),)),
            pltpu.SemaphoreType.DMA((split,)),
        ],
    )[0]


def solution(mesh):
    return jax.shard_map(
        on_device,
        mesh=mesh,
        in_specs=(
            P(("groups", "seq"), "head"),
            P(None, "head"),
            P(None, "head"),
            P(None, "head"),
            P("head", None),
            P(None, ("groups", "seq")),
            P("head"),
        ),
        out_specs=P(("groups", "seq"), "head"),
        check_vma=False,
    )
```
